128 devices in a mesh: layer: 16 (over x, y_hi, core), row: 8 (over y_lo, z).
Axes of the slice: x: 4, y: 4 (y_hi: 2, y_lo: 2; y = y_hi * 2 + y_lo), z: 4, core: 2. Of those that a mesh axis runs over, the one named last changes fastest.
Arguments:
- green: bfloat16 [16, 8192, 8192], P('layer', 'row'), may hold values from -0.09375 to 0.09375
- source_traces: bfloat16 [16, 128, 8192], P('layer', None, 'row'), may hold values from -6 to 6
Outputs:
- traces: bfloat16 [16, 128, 8192], P('layer', None, 'row')
The draws below stay inside these ranges and needn't reach their ends.
All inputs are finite; a program needn't handle non-finite values.
Results may differ from the reference program's by a relative error of at most 0.007.
Values may be sent and summed in bfloat16 or wider, within the bound.
No kernel may reach another device: no remote copies, remote signals or barrier semaphores. Data moves between devices by JAX's collectives and lax.ppermute only.
A program may use at most 128 MiB of HBM per device.

```python
import jax
import jax.numpy as jnp
from jax import lax

M = 8192
S = 64
ITERS = 4
LAYERS = 16


def spiked(array, key, source, target, shards_of, factor):
    def block_of(position):
        return (jnp.arange(array.shape[position]) // (array.shape[position] // shards_of)).reshape((-1,) + (1,) * (array.ndim - 1 - position))

    near = jax.random.permutation(key, shards_of)[block_of(target)]
    second = (block_of(target) + shards_of // 2) % shards_of
    return jnp.where((block_of(source) == near) | (block_of(source) == second), factor * array, array)


def block_levels(key, dims, pieces, low, top_value):
    level = 1.0
    for position, parts in pieces:
        steps = jax.random.uniform(jax.random.fold_in(jax.random.fold_in(key, 6), position), (parts,), jnp.float32, low / len(pieces), top_value / len(pieces))
        level = level * jnp.repeat(jnp.exp(steps), dims[position] // parts).reshape((-1,) + (1,) * (len(dims) - 1 - position))
    return level


def normal_values(rng, dims, width, limit, cuts=(), held_as=jnp.bfloat16):
    loudness = block_levels(rng, dims, cuts, -0.22, 0.18) if cuts else 1.0
    entries = jax.random.normal(rng, dims, jnp.float32) * width * loudness
    return jnp.minimum(jnp.maximum(entries, -limit), limit).astype(held_as)


def bell_draw_with(stream_key, shape, scale, most, shards, heavy, dtype=jnp.bfloat16):
    drawn = scale * jax.random.normal(stream_key, shape, jnp.float32)
    if shards:
        drawn = drawn * block_levels(stream_key, shape, shards, -0.22, 0.18)
    return jnp.clip(spiked(drawn, jax.random.fold_in(stream_key, 3), *heavy), -most, most).astype(dtype)


def setup_inputs(seed: int = 0) -> dict:
    splits = jax.random.split(jax.random.key(seed), 3)
    return {
        "green": bell_draw_with(splits[0], (LAYERS, M, M), M ** -0.5, 0.09375, ((0, 16), (1, 8)), (1, 2, 8, 2.0)),
        "source_traces": normal_values(splits[1], (LAYERS, 2 * S, M), 1.0, 6.0, ((0, 16), (2, 8))),
    }


def apply_layer(pair):
    incoming, matrix = pair
    return jnp.dot(incoming, matrix, preferred_element_type=jnp.float32)


def reference(green, source_traces):
    traces = source_traces
    half = source_traces.shape[1] // 2
    for step in range(ITERS):
        zero_block = jnp.zeros((1, half, M), jnp.bfloat16)
        down_in = jnp.concatenate([zero_block, traces[:-1, :half]], axis=0)
        up_in = jnp.concatenate([traces[1:, half:], zero_block], axis=0)
        incoming = jnp.concatenate([down_in, up_in], axis=1)
        applied = lax.map(apply_layer, (incoming, green))
        traces = (source_traces.astype(jnp.float32) + applied).astype(jnp.bfloat16)
    return traces
```

```python
import jax
import jax.numpy as jnp
from jax import lax
from jax.experimental import pallas as pl
from jax.experimental.pallas import tpu as pltpu
from jax.sharding import PartitionSpec as P

ITERS = 4
BF16 = jnp.bfloat16
F32 = jnp.float32
VMEM = pl.BlockSpec(memory_space=pltpu.VMEM)


def call(kernel, name, outs, *args):
    return pl.pallas_call(
        kernel,
        in_specs=[VMEM] * len(args),
        out_specs=[VMEM] * len(outs),
        out_shape=[pltpu.VMEM(shape, dtype) for shape, dtype in outs],
        compiler_params=pltpu.CompilerParams(vmem_limit_bytes=8 << 20),
        name=name,
    )(*args)


def even_layer():
    return lax.rem(lax.axis_index("layer"), 2) == 0


def split_kernel(s_ref, far_ref, near_ref):
    half = far_ref.shape[0]

    @pl.when(even_layer())
    def _():
        far_ref[...] = s_ref[half:]
        near_ref[...] = s_ref[:half]

    @pl.when(jnp.logical_not(even_layer()))
    def _():
        far_ref[...] = s_ref[:half]
        near_ref[...] = s_ref[half:]


def product(x, g_ref, target, width):
    block = lax.axis_index("row") ^ target
    return jnp.dot(x, g_ref[:, pl.ds(pl.multiple_of(block * width, width), width)], preferred_element_type=F32)


def first_kernel(a_ref, b_ref, g_ref, send_a_ref, send_b_ref, keep_b_ref):
    half, width = a_ref.shape
    x = jnp.concatenate([a_ref[...], b_ref[...]], axis=0)
    for i, target in enumerate((2, 6, 1, 5)):
        out = product(x, g_ref, target, width)
        send_a_ref[i] = out[:half].astype(BF16)
        if i < 2:
            send_b_ref[i] = out[half:].astype(BF16)
        else:
            keep_b_ref[i - 2] = out[half:]


def second_kernel(a_ref, b_ref, g_ref, part_ref, send_b_ref, keep_a_ref):
    half, width = a_ref.shape
    x = jnp.concatenate([a_ref[...], b_ref[...]], axis=0)
    send_b_ref[:2] = part_ref[...]
    for i, target in enumerate((3, 7)):
        out = product(x, g_ref, target, width)
        keep_a_ref[i] = out[:half]
        send_b_ref[2 + i] = out[half:].astype(BF16)


def third_kernel(a_ref, b_ref, g_ref, own_a_ref, own_b_ref):
    half, width = a_ref.shape
    x = jnp.concatenate([a_ref[...], b_ref[...]], axis=0)
    for i, target in enumerate((0, 4)):
        out = product(x, g_ref, target, width)
        own_a_ref[i] = out[:half]
        own_b_ref[i] = out[half:]


def merge_kernel(keep_ref, got_ref, send_ref):
    for i in range(2):
        send_ref[i] = (keep_ref[i] + got_ref[i].astype(F32)).astype(BF16)


def merge_again_kernel(own_ref, got_ref, again_ref, send_ref):
    send_ref[...] = (own_ref[1] + got_ref[3].astype(F32) + again_ref[1].astype(F32)).astype(BF16)


def total_of(s_ref, own_ref, got_ref, again_ref, last_ref):
    total = own_ref[0] + got_ref[2].astype(F32) + again_ref[0].astype(F32) + last_ref[...].astype(F32)
    return (s_ref[...].astype(F32) + total).astype(BF16)


def sum_kernel(s_ref, own_ref, got_ref, again_ref, last_ref, out_ref):
    out_ref[...] = total_of(s_ref, own_ref, got_ref, again_ref, last_ref)


def join_kernel(*refs):
    out_ref = refs[-1]
    half = out_ref.shape[0] // 2
    a = total_of(*refs[:5])
    b = total_of(*refs[5:10])

    @pl.when(even_layer())
    def _():
        out_ref[:half] = b
        out_ref[half:] = a

    @pl.when(jnp.logical_not(even_layer()))
    def _():
        out_ref[:half] = a
        out_ref[half:] = b


def far_swap(block):
    pairs = [(i, i + 1) for i in range(1, lax.axis_size("layer") - 1, 2)]
    return lax.ppermute(block, "layer", pairs + [(j, i) for i, j in pairs])


def near_swap(block):
    return lax.ppermute(block, "layer", [(i, i ^ 1) for i in range(lax.axis_size("layer"))])


def swapped(block, k):
    return lax.ppermute(block, "row", [(i, i ^ k) for i in range(8)])


def local(green, source_traces):
    s = source_traces[0]
    g = green[0]
    rows, width = s.shape
    half = rows // 2
    piece = ((half, width), BF16)
    two = ((2, half, width), BF16)
    four = ((4, half, width), BF16)
    two_wide = ((2, half, width), F32)
    s_a, s_b = call(split_kernel, "split", [piece, piece], s)
    out_a, out_b = s_a, s_b
    for step in range(ITERS):
        in_b = far_swap(out_a)
        in_a = near_swap(out_b)
        send_a, part_b, keep_b = call(first_kernel, "first", [four, two, two_wide], in_a, in_b, g)
        got_a = swapped(send_a, 1)
        send_b, keep_a = call(second_kernel, "second", [four, two_wide], in_a, in_b, g, part_b)
        got_b = swapped(send_b, 3)
        own_a, own_b = call(third_kernel, "third", [two_wide, two_wide], in_a, in_b, g)
        send_a, = call(merge_kernel, "merge", [two], keep_a, got_a)
        again_a = swapped(send_a, 3)
        send_b, = call(merge_kernel, "merge", [two], keep_b, got_b)
        again_b = swapped(send_b, 1)
        send_a, = call(merge_again_kernel, "merge_again", [piece], own_a, got_a, again_a)
        last_a = swapped(send_a, 4)
        send_b, = call(merge_again_kernel, "merge_again", [piece], own_b, got_b, again_b)
        last_b = swapped(send_b, 4)
        if step < ITERS - 1:
            out_a, = call(sum_kernel, "sum", [piece], s_a, own_a, got_a, again_a, last_a)
            out_b, = call(sum_kernel, "sum", [piece], s_b, own_b, got_b, again_b, last_b)
    out, = call(join_kernel, "join", [((rows, width), BF16)], s_a, own_a, got_a, again_a, last_a, s_b, own_b, got_b, again_b, last_b)
    return out[None]


def solution(mesh):
    return jax.shard_map(
        local,
        mesh=mesh,
        in_specs=(P("layer", "row", None), P("layer", None, "row")),
        out_specs=P("layer", None, "row"),
        check_vma=False,
    )
```
